32 devices in a mesh: seq: 8 (over y, x, core), head: 4 (over z).
Axes of the slice: x: 2, y: 2, z: 4, core: 2. Of those that a mesh axis runs over, the one named last changes fastest.
Arguments:
- frames: bfloat16 [8192, 1024], P(('seq', 'head')), may hold values from -6 to 6
- cotangent: bfloat16 [8192, 1024], P(('seq', 'head')), may hold values from -6 to 6
- norm_gain: float32 [1024], replicated, may hold values from 0.25 to 1.75
- w_qkv: bfloat16 [3, 1024, 1024], replicated
- w_out: bfloat16 [1024, 1024], replicated, may hold values from -0.1875 to 0.1875
Outputs:
- output: bfloat16 [8192, 1024], P(('seq', 'head'))
- grad_frames: bfloat16 [8192, 1024], P(('seq', 'head'))
- grad_qkv: float32 [3, 1024, 1024], P(None, 'seq', 'head')
- grad_out: float32 [1024, 1024], P('seq', 'head')
The draws below stay inside these ranges and needn't reach their ends.
All inputs are finite; a program needn't handle non-finite values.
Results may differ from the reference program's by a relative error of at most 0.015.
Values may be sent and summed in bfloat16 or wider, within the bound.
A program may use at most 128 MiB of HBM per device.

```python
import jax
import jax.numpy as jnp
from jax import lax

D = 1024
HEAD_SIZE = 128
WINDOW = 128
FRAMES = 8192


def draw_w_qkv(key, part):
    base = jax.random.normal(key, (3, D, D), jnp.float32) * D ** (-0.5)
    return base.astype(jnp.bfloat16)


def spiked(array, own_key, source, target, parts, factor):
    def block_of(position):
        return (jnp.arange(array.shape[position]) // (array.shape[position] // parts)).reshape((-1,) + (1,) * (array.ndim - 1 - position))

    one_side = jax.random.permutation(own_key, parts)[block_of(target)]
    second = (block_of(target) + parts // 2) % parts
    return jnp.where((block_of(source) == one_side) | (block_of(source) == second), factor * array, array)


def levels(own_key, dims, pieces, low, top_value):
    level = 1.0
    for position, blocks in pieces:
        draws = jax.random.uniform(jax.random.fold_in(jax.random.fold_in(own_key, 6), position), (blocks,), jnp.float32, low / len(pieces), top_value / len(pieces))
        level = level * jnp.repeat(jnp.exp(draws), dims[position] // blocks).reshape((-1,) + (1,) * (len(dims) - 1 - position))
    return level


def scatter_about(key, extent, deviation, reach, cuts=(), kind=jnp.bfloat16):
    result = deviation * jax.random.normal(key, extent, jnp.float32)
    if cuts:
        result = result * levels(key, extent, cuts, -0.22, 0.18)
    return jnp.clip(result, -reach, reach).astype(kind)


def gaussian_with(own_key, dims, spread, reach, pieces, heavy, kind=jnp.bfloat16):
    entries = spread * jax.random.normal(own_key, dims, jnp.float32)
    if pieces:
        entries = entries * levels(own_key, dims, pieces, -0.22, 0.18)
    return jnp.clip(spiked(entries, jax.random.fold_in(own_key, 3), *heavy), -reach, reach).astype(kind)


def setup_inputs(seed: int = 0) -> dict:
    splits = jax.random.split(jax.random.key(seed), 6)
    return {
        "frames": scatter_about(splits[0], (FRAMES, D), 1.0, 6.0, ((0, 32),)),
        "cotangent": gaussian_with(splits[1], (FRAMES, D), 1.0, 6.0, ((0, 32),), (0, 1, 32, 2.75)),
        "norm_gain": jnp.clip(1.0 + 0.15 * jax.random.normal(splits[2], (D,), jnp.float32), 0.25, 1.75),
        "w_qkv": draw_w_qkv(jax.random.fold_in(splits[5], 71), 0),
        "w_out": scatter_about(splits[4], (D, D), D ** -0.5, 0.1875),
    }


EPSILON = 1e-05
MASKED = -1e+30

def layer_norm(values, norm_gain):
    average = lax.optimization_barrier(jnp.mean(values, axis=-1, keepdims=True))
    centered = values - average
    variance = lax.optimization_barrier(jnp.mean(centered * centered, axis=-1, keepdims=True))
    return centered * lax.rsqrt(variance + EPSILON) * norm_gain

def norm_grad(frames, norm_gain, upstream):
    _, pullback = jax.vjp(lambda v: layer_norm(v, norm_gain), frames.astype(jnp.float32))
    return pullback(upstream.astype(jnp.float32))[0]

def attention(query_rows, key_rows, value_rows, offset, frame_total):
    length, channels = query_rows.shape
    head_count = channels // HEAD_SIZE
    block_rows = min(length, 512)
    block_count = length // block_rows
    key_span = block_rows + 2 * WINDOW
    score_scale = HEAD_SIZE ** (-0.5)

    def one_block(block_index):
        anchor = block_index * block_rows
        query_part = lax.dynamic_slice_in_dim(query_rows, anchor, block_rows, 0).reshape(block_rows, head_count, HEAD_SIZE)
        key_part = lax.dynamic_slice_in_dim(key_rows, anchor, key_span, 0).reshape(key_span, head_count, HEAD_SIZE)
        value_part = lax.dynamic_slice_in_dim(value_rows, anchor, key_span, 0).reshape(key_span, head_count, HEAD_SIZE)
        query_pos = offset + anchor + jnp.arange(block_rows, dtype=jnp.int32)
        key_pos = offset + anchor - WINDOW + jnp.arange(key_span, dtype=jnp.int32)
        distance = query_pos[:, None] - key_pos[None, :]
        allowed = (jnp.abs(distance) <= WINDOW) & (key_pos >= 0)[None, :] & (key_pos < frame_total)[None, :]
        scores = jnp.einsum('qhe,khe->hqk', query_part, key_part, precision=lax.Precision.HIGHEST) * score_scale
        scores = jnp.where(allowed[None], scores, MASKED)
        row_max = lax.stop_gradient(lax.optimization_barrier(jnp.max(scores, axis=-1, keepdims=True)))
        weights = jnp.exp(scores - row_max)
        weights = weights / lax.optimization_barrier(jnp.sum(weights, axis=-1, keepdims=True))
        combined = jnp.einsum('hqk,khe->qhe', weights, value_part, precision=lax.Precision.HIGHEST)
        return combined.reshape(block_rows, channels)
    results = lax.map(jax.checkpoint(one_block), jnp.arange(block_count, dtype=jnp.int32))
    return results.reshape(length, channels)

def attention_grad(query_rows, key_rows, value_rows, offset, frame_total, upstream):
    _, pullback = jax.vjp(lambda a, b, c: attention(a, b, c, offset, frame_total), query_rows, key_rows, value_rows)
    return pullback(upstream.astype(jnp.float32))

def reference(frames, cotangent, norm_gain, w_qkv, w_out):
    frame_total = frames.shape[0]
    grad_scale = frame_total ** (-0.5)
    normed = layer_norm(frames.astype(jnp.float32), norm_gain).astype(jnp.bfloat16)
    projected = jnp.stack([jnp.dot(normed, w_qkv[member], preferred_element_type=jnp.float32) for member in range(3)]).astype(jnp.bfloat16)
    query_rows = projected[0].astype(jnp.float32)
    key_rows = jnp.pad(projected[1].astype(jnp.float32), ((WINDOW, WINDOW), (0, 0)))
    value_rows = jnp.pad(projected[2].astype(jnp.float32), ((WINDOW, WINDOW), (0, 0)))
    anchor = jnp.zeros((), jnp.int32)
    attended = attention(query_rows, key_rows, value_rows, anchor, frame_total).astype(jnp.bfloat16)
    output = (frames.astype(jnp.float32) + jnp.dot(attended, w_out, preferred_element_type=jnp.float32)).astype(jnp.bfloat16)
    grad_attended = jnp.dot(cotangent, w_out.T, preferred_element_type=jnp.float32).astype(jnp.bfloat16)
    grad_out = jnp.dot(attended.T, cotangent, preferred_element_type=jnp.float32) * grad_scale
    grad_query, grad_keys, grad_values = attention_grad(query_rows, key_rows, value_rows, anchor, frame_total, grad_attended)
    grad_proj = jnp.stack([grad_query, grad_keys[WINDOW:WINDOW + frame_total], grad_values[WINDOW:WINDOW + frame_total]]).astype(jnp.bfloat16)
    grad_sum = jnp.dot(grad_proj[0], w_qkv[0].T, preferred_element_type=jnp.float32)
    grad_sum = grad_sum + jnp.dot(grad_proj[1], w_qkv[1].T, preferred_element_type=jnp.float32)
    grad_sum = grad_sum + jnp.dot(grad_proj[2], w_qkv[2].T, preferred_element_type=jnp.float32)
    grad_normed = grad_sum.astype(jnp.bfloat16)
    grad_frames = (cotangent.astype(jnp.float32) + norm_grad(frames, norm_gain, grad_normed)).astype(jnp.bfloat16)
    grad_qkv = jnp.stack([jnp.dot(normed.T, grad_proj[member], preferred_element_type=jnp.float32) for member in range(3)]) * grad_scale
    return (output, grad_frames, grad_qkv, grad_out)
```

```python
import functools

import jax
import jax.numpy as jnp
from jax import lax
from jax.experimental import pallas as pl
from jax.experimental.pallas import tpu as pltpu
from jax.sharding import PartitionSpec as P

HEAD_SIZE = 128
WINDOW = 128

EPSILON = 1e-05
MASKED = -1e30
AXES = ("seq", "head")


def layer_norm(values, norm_gain):
    average = jnp.mean(values, axis=-1, keepdims=True)
    centered = values - average
    variance = jnp.mean(centered * centered, axis=-1, keepdims=True)
    return centered * lax.rsqrt(variance + EPSILON) * norm_gain


def norm_grad(frames, norm_gain, upstream):
    _, pullback = jax.vjp(lambda v: layer_norm(v, norm_gain), frames.astype(jnp.float32))
    return pullback(upstream.astype(jnp.float32))[0]


def shift(rows, step):
    devices = lax.axis_size("seq") * lax.axis_size("head")
    pairs = [(i, i + step) for i in range(devices) if 0 <= i + step < devices]
    return lax.ppermute(rows, AXES, pairs)


def dot(a, b, contract):
    return lax.dot_general(a, b, (contract, ((), ())), preferred_element_type=jnp.float32)


def attention_kernel(heads, offset_ref, q_ref, k_ref, v_ref, up_ref, out_ref, dq_ref, mid_ref, edge_ref):
    length = q_ref.shape[0]
    blocks = length // WINDOW
    span = 3 * WINDOW
    scale = HEAD_SIZE ** (-0.5)
    offset, total = offset_ref[0], offset_ref[1]
    row = lax.broadcasted_iota(jnp.int32, (WINDOW, span), 0)
    col = lax.broadcasted_iota(jnp.int32, (WINDOW, span), 1)
    near = (col >= row) & (col <= row + 2 * WINDOW)
    for head in range(heads):
        lanes = slice(head * HEAD_SIZE, (head + 1) * HEAD_SIZE)
        key_grads = [None] * (blocks + 2)
        value_grads = [None] * (blocks + 2)
        for block in range(blocks):
            rows = slice(block * WINDOW, (block + 1) * WINDOW)
            keys = slice(block * WINDOW, block * WINDOW + span)
            q, k, v = q_ref[rows, lanes], k_ref[keys, lanes], v_ref[keys, lanes]
            up = up_ref[rows, lanes]
            position = offset + (block - 1) * WINDOW + col
            allowed = near & (position >= 0) & (position < total)
            scores = jnp.where(allowed, dot(q, k, ((1,), (1,))) * scale, MASKED)
            weights = jnp.exp(scores - jnp.max(scores, axis=-1, keepdims=True))
            weights = weights / jnp.sum(weights, axis=-1, keepdims=True)
            rounded = weights.astype(jnp.bfloat16)
            out_ref[rows, lanes] = dot(rounded, v, ((1,), (0,))).astype(jnp.bfloat16)
            grad = dot(up, v, ((1,), (1,)))
            centre = jnp.sum(weights * grad, axis=-1, keepdims=True)
            grad = (weights * (grad - centre) * scale).astype(jnp.bfloat16)
            dq_ref[rows, lanes] = dot(grad, k, ((1,), (0,))).astype(jnp.bfloat16)
            key_grad = dot(grad, q, ((0,), (0,)))
            value_grad = dot(rounded, up, ((0,), (0,)))
            for part in range(3):
                piece = slice(part * WINDOW, (part + 1) * WINDOW)
                for sums, term in ((key_grads, key_grad[piece]), (value_grads, value_grad[piece])):
                    held = sums[block + part]
                    sums[block + part] = term if held is None else held + term
        for which, sums in enumerate((key_grads, value_grads)):
            edge_ref[which, :WINDOW, lanes] = sums[0].astype(jnp.bfloat16)
            edge_ref[which, WINDOW:, lanes] = sums[-1].astype(jnp.bfloat16)
            for block in range(blocks):
                mid_ref[which, block * WINDOW : (block + 1) * WINDOW, lanes] = sums[block + 1]


def attention(query, key, value, upstream, offset, total):
    length, channels = query.shape
    heads = 2
    wide = heads * HEAD_SIZE
    bordered = key.shape[0]

    def rows_spec(rows):
        return pl.BlockSpec((rows, wide), lambda i: (0, i))

    def pair_spec(rows):
        return pl.BlockSpec((2, rows, wide), lambda i: (0, 0, i))

    return pl.pallas_call(
        functools.partial(attention_kernel, heads),
        grid=(channels // wide,),
        in_specs=[
            pl.BlockSpec(memory_space=pltpu.SMEM),
            rows_spec(length),
            rows_spec(bordered),
            rows_spec(bordered),
            rows_spec(length),
        ],
        out_specs=[rows_spec(length), rows_spec(length), pair_spec(length), pair_spec(2 * WINDOW)],
        out_shape=[
            jax.ShapeDtypeStruct((length, channels), jnp.bfloat16),
            jax.ShapeDtypeStruct((length, channels), jnp.bfloat16),
            jax.ShapeDtypeStruct((2, length, channels), jnp.float32),
            jax.ShapeDtypeStruct((2, 2 * WINDOW, channels), jnp.bfloat16),
        ],
        name="attention",
    )(jnp.stack([offset, jnp.int32(total)]), query, key, value, upstream)


def bits_of(size):
    return list(range(size.bit_length() - 1))


def scatter_kernel(chunks, orders, sizes, scale, *refs):
    left, right = refs[:chunks], refs[chunks : 2 * chunks]
    out_ref, held, landed, send_sem, recv_sem = refs[2 * chunks :]
    seq_size, head_size = sizes
    tiles = seq_size * head_size
    place = {axis: lax.axis_index(axis) for axis in AXES}
    stages = len(orders[0])
    tile_rows, tile_cols = held.shape[2:]

    def bit_at(order):
        axis, bit = order
        return (place[axis] // 2**bit) % 2

    def partner(order):
        axis, bit = order
        moved = place[axis] + (1 - 2 * bit_at(order)) * 2**bit
        return tuple(moved if name == axis else place[name] for name in AXES)

    barrier = pltpu.get_barrier_semaphore()
    for order in orders[0]:
        pl.semaphore_signal(
            barrier, inc=1, device_id=partner(order), device_id_type=pl.DeviceIdType.MESH
        )
    pl.semaphore_wait(barrier, stages)

    def base(chunk, stage):
        total = 0
        for step in range(stage):
            total = total + bit_at(orders[chunk][step]) * (tiles >> (step + 1))
        return total

    def landing(stage):
        return tiles - (tiles >> stage)

    def copy(chunk, stage):
        half = tiles >> (stage + 1)
        order = orders[chunk][stage]
        other = base(chunk, stage) + (1 - bit_at(order)) * half
        return pltpu.make_async_remote_copy(
            src_ref=held.at[chunk, pl.ds(other, half)],
            dst_ref=landed.at[chunk, pl.ds(landing(stage), half)],
            send_sem=send_sem.at[chunk, stage],
            recv_sem=recv_sem.at[chunk, stage],
            device_id=partner(order),
            device_id_type=pl.DeviceIdType.MESH,
        )

    def finish(chunk, stage):
        copy(chunk, stage).wait()
        half = tiles >> (stage + 1)
        keep = base(chunk, stage + 1)
        if stage == stages - 1:
            own = held[chunk, keep].astype(jnp.float32)
            own = own + landed[chunk, landing(stage)].astype(jnp.float32)
            out_ref[chunk] = own * scale
            return

        def add(step, carry):
            own = held[chunk, keep + step].astype(jnp.float32)
            own = own + landed[chunk, landing(stage) + step].astype(jnp.float32)
            held[chunk, keep + step] = own.astype(jnp.bfloat16)
            return carry

        lax.fori_loop(0, half, add, 0)

    def column_place(chunk, col):
        total = 0
        for step, (axis, bit) in enumerate(orders[chunk]):
            if axis == "head":
                total += ((col >> bit) & 1) * (tiles >> (step + 1))
        return total

    def multiply(chunk, half):
        seq_steps = [bit for axis, bit in orders[chunk] if axis == "seq"]

        def one(step, carry):
            slot = half * (seq_size // 2) + step
            row_block = 0
            for depth, bit in enumerate(seq_steps):
                row_block = row_block + ((slot // (seq_size >> (depth + 1))) % 2) * 2**bit
            product = dot(left[chunk][row_block], right[chunk][...], ((1,), (0,))).astype(jnp.bfloat16)
            for col in range(head_size):
                held[chunk, slot * head_size + column_place(chunk, col)] = product[
                    :, col * tile_cols : (col + 1) * tile_cols
                ]
            return carry

        lax.fori_loop(0, seq_size // 2, one, 0)

    for wave in range(chunks + stages):
        for chunk in range(chunks - 1, -1, -1):
            stage = wave - chunk
            if stage == 0:
                mine = bit_at(orders[chunk][0])
                multiply(chunk, 1 - mine)
                copy(chunk, 0).start()
                multiply(chunk, mine)
            elif 0 < stage <= stages:
                finish(chunk, stage - 1)
                if stage < stages:
                    copy(chunk, stage).start()


def scatter_products(left, right, collective_id, scale):
    seq_size, head_size = lax.axis_size("seq"), lax.axis_size("head")
    chunks = len(left)
    depth, cols = right[0].shape
    rows = left[0].shape[0]
    tile_rows, tile_cols = rows // seq_size, cols // head_size
    tiles = seq_size * head_size
    seq_bits, head_bits = bits_of(seq_size), bits_of(head_size)
    tail = [("head", bit) for bit in reversed(head_bits)]
    orders = []
    for chunk in range(chunks):
        outer = seq_bits[1:] if chunk % 2 == 0 else seq_bits[:0:-1]
        orders.append([("seq", bit) for bit in seq_bits[:1] + outer] + tail)
    stages = len(orders[0])
    blocks = [term.reshape(seq_size, tile_rows, depth) for term in left]
    vmem = pl.BlockSpec(memory_space=pltpu.VMEM)
    return pl.pallas_call(
        functools.partial(scatter_kernel, chunks, orders, (seq_size, head_size), scale),
        out_shape=jax.ShapeDtypeStruct((chunks, tile_rows, tile_cols), jnp.float32),
        in_specs=[vmem] * (2 * chunks),
        out_specs=vmem,
        scratch_shapes=[
            pltpu.VMEM((chunks, tiles, tile_rows, tile_cols), jnp.bfloat16),
            pltpu.VMEM((chunks, tiles, tile_rows, tile_cols), jnp.bfloat16),
            pltpu.SemaphoreType.DMA((chunks, stages)),
            pltpu.SemaphoreType.DMA((chunks, stages)),
        ],
        compiler_params=pltpu.CompilerParams(collective_id=collective_id, has_side_effects=True),
        cost_estimate=pl.CostEstimate(
            flops=2 * chunks * rows * depth * cols,
            bytes_accessed=20 * chunks * rows * cols,
            transcendentals=0,
        ),
        name="scatter_products_%d" % collective_id,
    )(*blocks, *right)


def shards(frames, cotangent, norm_gain, w_qkv, w_out):
    length = frames.shape[0]
    position = lax.axis_index("seq") * lax.axis_size("head") + lax.axis_index("head")
    frame_total = lax.axis_size("seq") * lax.axis_size("head") * length
    grad_scale = frame_total ** (-0.5)
    before = shift(frames[length - WINDOW :], 1)
    after = shift(frames[:WINDOW], -1)
    upstream = dot(cotangent, w_out, ((1,), (1,))).astype(jnp.bfloat16)
    bordered = jnp.concatenate([before, frames, after], axis=0)
    normed_all = layer_norm(bordered.astype(jnp.float32), norm_gain).astype(jnp.bfloat16)
    normed = normed_all[WINDOW : WINDOW + length]
    query = dot(normed, w_qkv[0], ((1,), (0,))).astype(jnp.bfloat16)
    key = dot(normed_all, w_qkv[1], ((1,), (0,))).astype(jnp.bfloat16)
    value = dot(normed_all, w_qkv[2], ((1,), (0,))).astype(jnp.bfloat16)
    attended, grad_query, pair_grads, edges = attention(
        query, key, value, upstream, position * length, frame_total
    )
    from_next = shift(edges[:, :WINDOW], -1)
    from_previous = shift(edges[:, WINDOW:], 1)
    normed_t = normed.T
    first = scatter_products([attended.T, normed_t], [cotangent, grad_query], 0, grad_scale)
    output = (frames.astype(jnp.float32) + dot(attended, w_out, ((1,), (0,)))).astype(jnp.bfloat16)
    pair_grads = pair_grads.at[:, :WINDOW].add(from_previous.astype(jnp.float32))
    pair_grads = pair_grads.at[:, length - WINDOW :].add(from_next.astype(jnp.float32))
    grad_key, grad_value = pair_grads[0].astype(jnp.bfloat16), pair_grads[1].astype(jnp.bfloat16)
    second = scatter_products([normed_t, normed_t], [grad_key, grad_value], 1, grad_scale)
    grad_normed = (
        dot(grad_query, w_qkv[0], ((1,), (1,)))
        + dot(grad_key, w_qkv[1], ((1,), (1,)))
        + dot(grad_value, w_qkv[2], ((1,), (1,)))
    ).astype(jnp.bfloat16)
    grad_frames = (
        cotangent.astype(jnp.float32) + norm_grad(frames, norm_gain, grad_normed)
    ).astype(jnp.bfloat16)
    grad_qkv = jnp.concatenate([first[1:], second], axis=0)
    return (output, grad_frames, grad_qkv, first[0])


def solution(mesh):
    in_specs = (P(("seq", "head"), None), P(("seq", "head"), None), P(), P(), P())
    out_specs = (
        P(("seq", "head"), None),
        P(("seq", "head"), None),
        P(None, "seq", "head"),
        P("seq", "head"),
    )
    return jax.shard_map(shards, mesh=mesh, in_specs=in_specs, out_specs=out_specs, check_vma=False)
```

```python
import functools

import jax
import jax.numpy as jnp
from jax import lax
from jax.experimental import pallas as pl
from jax.experimental.pallas import tpu as pltpu
from jax.sharding import PartitionSpec as P

HEAD_SIZE = 128
WINDOW = 128

EPSILON = 1e-05
MASKED = -1e30
AXES = ("seq", "head")


def dot(a, b, contract):
    return lax.dot_general(a, b, (contract, ((), ())), preferred_element_type=jnp.float32)


def bits_of(size):
    return list(range(size.bit_length() - 1))


def block_kernel(
    sizes, orders, scale,
    frames, cotangent, gain, w_qkv_hbm, w_out_hbm,
    output, grad_frames, grad_qkv, grad_out,
    w_qkv, w_out, normed, normed_t, query, key, value, upstream, attended, attended_t,
    grad_query, mid, edge_out, edge_in, grad_pair, grad_normed, held, landed, halo,
    weight_sem, halo_send, halo_recv, edge_send, edge_recv, send_sem, recv_sem,
):
    seq_size, head_size = sizes
    devices = tiles = seq_size * head_size
    length, channels = frames.shape
    chunks, stages = len(orders), len(orders[0])
    tile_rows, tile_cols = held.shape[2:]
    place = {axis: lax.axis_index(axis) for axis in AXES}
    position = place["seq"] * head_size + place["head"]
    bf16, f32 = jnp.bfloat16, jnp.float32
    strip = min(256, channels)

    def neighbour(step):
        there = (position + step + devices) % devices
        return (there // head_size, there % head_size)

    def bit_at(order):
        axis, bit = order
        return (place[axis] // 2**bit) % 2

    def partner(order):
        axis, bit = order
        moved = place[axis] + (1 - 2 * bit_at(order)) * 2**bit
        return tuple(moved if name == axis else place[name] for name in AXES)

    weights = [pltpu.make_async_copy(w_out_hbm, w_out, weight_sem.at[3])]
    for which in range(3):
        weights.append(
            pltpu.make_async_copy(w_qkv_hbm.at[which], w_qkv.at[which], weight_sem.at[which])
        )
    for one in weights:
        one.start()

    greeted = [partner(order) for order in orders[0]] + [neighbour(1), neighbour(-1)]
    barrier = pltpu.get_barrier_semaphore()
    for device in greeted:
        pl.semaphore_signal(barrier, inc=1, device_id=device, device_id_type=pl.DeviceIdType.MESH)
    pl.semaphore_wait(barrier, len(greeted))

    def halo_copy(side):
        rows = pl.ds(length - WINDOW, WINDOW) if side == 0 else pl.ds(0, WINDOW)
        return pltpu.make_async_remote_copy(
            src_ref=frames.at[rows],
            dst_ref=halo.at[side],
            send_sem=halo_send.at[side],
            recv_sem=halo_recv.at[side],
            device_id=neighbour(1 if side == 0 else -1),
            device_id_type=pl.DeviceIdType.MESH,
        )

    halo_copy(0).start()
    halo_copy(1).start()

    def standardise(values):
        average = jnp.mean(values, axis=-1, keepdims=True)
        centered = values - average
        variance = jnp.mean(centered * centered, axis=-1, keepdims=True)
        inverse = lax.rsqrt(variance + EPSILON)
        return centered * inverse, inverse

    few = 64

    def norm_rows(source, target_row, rows):
        def one(step, carry):
            values = source[pl.ds(pl.multiple_of(step * few, few), few), :].astype(f32)
            rounded = (standardise(values)[0] * gain[...]).astype(bf16)
            normed[pl.ds(pl.multiple_of(target_row + step * few, few), few), :] = rounded
            return carry

        lax.fori_loop(0, rows // few, one, 0)

    def multiply_into(target, rows, left, weight, side):
        for start in range(0, channels, strip):
            cols = slice(start, start + strip)
            other = weight[:, cols] if side == 0 else weight[cols, :]
            target[rows, cols] = dot(left, other, ((1,), (side,))).astype(target.dtype)

    norm_rows(frames, WINDOW, length)
    own = slice(WINDOW, WINDOW + length)
    for start in range(0, length, 128):
        for col in range(0, channels, 128):
            tile = normed[WINDOW + start : WINDOW + start + 128, col : col + 128]
            normed_t[col : col + 128, start : start + 128] = tile.astype(f32).T.astype(bf16)
    weights[0].wait()
    everything = slice(0, length)
    multiply_into(upstream, everything, cotangent[...], w_out, 1)
    for which, target, rows in ((0, query, everything), (1, key, own), (2, value, own)):
        weights[1 + which].wait()
        multiply_into(target, rows, normed[own, :], w_qkv.at[which], 0)
    for side in range(2):
        halo_copy(side).wait()
        start = side * (length + WINDOW)
        norm_rows(halo.at[side], start, WINDOW)
    for side in range(2):
        start = side * (length + WINDOW)
        rows = slice(start, start + WINDOW)
        multiply_into(key, rows, normed[rows, :], w_qkv.at[1], 0)
        multiply_into(value, rows, normed[rows, :], w_qkv.at[2], 0)

    pairs, wide = edge_out.shape[0], edge_out.shape[-1]

    def edge_copy(pair, side):
        return pltpu.make_async_remote_copy(
            src_ref=edge_out.at[pair, side],
            dst_ref=edge_in.at[pair, side],
            send_sem=edge_send.at[pair, side],
            recv_sem=edge_recv.at[pair, side],
            device_id=neighbour(-1 if side == 0 else 1),
            device_id_type=pl.DeviceIdType.MESH,
        )

    blocks = length // WINDOW
    span = 3 * WINDOW
    score_scale = HEAD_SIZE ** (-0.5)
    row = lax.broadcasted_iota(jnp.int32, (WINDOW, span), 0)
    col = lax.broadcasted_iota(jnp.int32, (WINDOW, span), 1)
    near = (col >= row) & (col <= row + 2 * WINDOW)

    def attend(pair, carry):
        for head in range(wide // HEAD_SIZE):
            lane = pl.multiple_of(pair * wide + head * HEAD_SIZE, HEAD_SIZE)
            lanes = pl.ds(lane, HEAD_SIZE)
            here = slice(head * HEAD_SIZE, (head + 1) * HEAD_SIZE)
            key_grads = [None] * (blocks + 2)
            value_grads = [None] * (blocks + 2)
            for block in range(blocks):
                rows = slice(block * WINDOW, (block + 1) * WINDOW)
                keys = slice(block * WINDOW, block * WINDOW + span)
                q, k, v, up = query[rows, lanes], key[keys, lanes], value[keys, lanes], upstream[rows, lanes]
                frame = position * length + (block - 1) * WINDOW + col
                allowed = near & (frame >= 0) & (frame < devices * length)
                scores = jnp.where(allowed, dot(q, k, ((1,), (1,))) * score_scale, MASKED)
                share = jnp.exp(scores - jnp.max(scores, axis=-1, keepdims=True))
                share = share * (1.0 / jnp.sum(share, axis=-1, keepdims=True))
                rounded = share.astype(bf16)
                mixed = dot(rounded, v, ((1,), (0,)))
                attended[rows, lanes] = mixed.astype(bf16)
                attended_t[lanes, rows] = mixed.T.astype(bf16)
                grad = dot(up, v, ((1,), (1,)))
                centre = jnp.sum(share * grad, axis=-1, keepdims=True)
                grad = (share * (grad - centre) * score_scale).astype(bf16)
                grad_query[rows, lanes] = dot(grad, k, ((1,), (0,))).astype(bf16)
                key_grad = dot(grad, q, ((0,), (0,)))
                value_grad = dot(rounded, up, ((0,), (0,)))
                for part in range(3):
                    piece = slice(part * WINDOW, (part + 1) * WINDOW)
                    for sums, term in ((key_grads, key_grad[piece]), (value_grads, value_grad[piece])):
                        before = sums[block + part]
                        sums[block + part] = term if before is None else before + term
            for which, sums in enumerate((key_grads, value_grads)):
                edge_out[pair, 0, which, :, here] = sums[0].astype(bf16)
                edge_out[pair, 1, which, :, here] = sums[-1].astype(bf16)
                for block in range(blocks):
                    rows = slice(block * WINDOW, (block + 1) * WINDOW)
                    mid[which, rows, lanes] = sums[block + 1]
        edge_copy(pair, 0).start()
        edge_copy(pair, 1).start()
        return carry

    lax.fori_loop(0, pairs, attend, 0)

    def base(chunk, stage):
        total = 0
        for step in range(stage):
            total = total + bit_at(orders[chunk][step]) * (tiles >> (step + 1))
        return total

    def landing(stage):
        return tiles - (tiles >> stage)

    def copy(chunk, stage):
        half = tiles >> (stage + 1)
        order = orders[chunk][stage]
        other = base(chunk, stage) + (1 - bit_at(order)) * half
        return pltpu.make_async_remote_copy(
            src_ref=held.at[chunk, pl.ds(other, half)],
            dst_ref=landed.at[chunk, pl.ds(landing(stage), half)],
            send_sem=send_sem.at[chunk, stage],
            recv_sem=recv_sem.at[chunk, stage],
            device_id=partner(order),
            device_id_type=pl.DeviceIdType.MESH,
        )

    def advance(chunk, stage):
        copy(chunk, stage).wait()
        half = tiles >> (stage + 1)
        keep = base(chunk, stage + 1)
        if stage == stages - 1:
            total = held[chunk, keep].astype(f32) + landed[chunk, landing(stage)].astype(f32)
            if chunk == 0:
                grad_out[...] = total * scale
            else:
                grad_qkv[chunk - 1] = total * scale
            return

        def add(step, carry):
            total = held[chunk, keep + step].astype(f32) + landed[chunk, landing(stage) + step].astype(f32)
            held[chunk, keep + step] = total.astype(bf16)
            return carry

        lax.fori_loop(0, half, add, 0)
        copy(chunk, stage + 1).start()

    def tile_place(chunk, axis, index):
        total = 0
        for step, (name, bit) in enumerate(orders[chunk]):
            if name == axis:
                total = total + ((index // 2**bit) % 2) * (tiles >> (step + 1))
        return total

    def products(chunk, left, right, half):
        def one(step, carry):
            block = 2 * step + half
            rows = pl.ds(pl.multiple_of(block * tile_rows, tile_rows), tile_rows)
            product = dot(left[rows, :], right[...], ((1,), (0,))).astype(bf16)
            down = tile_place(chunk, "seq", block)
            for col in range(head_size):
                held[chunk, down + tile_place(chunk, "head", col)] = product[
                    :, col * tile_cols : (col + 1) * tile_cols
                ]
            return carry

        lax.fori_loop(0, seq_size // 2, one, 0)

    def launch(chunk, left, right):
        mine = bit_at(orders[chunk][0])
        products(chunk, left, right, 1 - mine)
        copy(chunk, 0).start()
        products(chunk, left, right, mine)

    launch(0, attended_t, cotangent)
    launch(1, normed_t, grad_query)
    advance(0, 0)
    advance(1, 0)
    for start in range(0, channels, strip):
        cols = slice(start, start + strip)
        mixed = dot(attended[...], w_out[:, cols], ((1,), (0,)))
        output[:, cols] = (frames[:, cols].astype(f32) + mixed).astype(bf16)
    multiply_into(grad_normed, everything, grad_query[...], w_qkv.at[0], 1)

    def combine(pair, carry):
        edge_copy(pair, 0).wait()
        edge_copy(pair, 1).wait()
        lanes = pl.ds(pl.multiple_of(pair * wide, wide), wide)
        last = length - WINDOW
        for which in range(2):
            first_rows = mid[which, :WINDOW, lanes] + edge_in[pair, 1, which].astype(f32)
            grad_pair[which, :WINDOW, lanes] = first_rows.astype(bf16)
            last_rows = mid[which, last:, lanes] + edge_in[pair, 0, which].astype(f32)
            grad_pair[which, last:, lanes] = last_rows.astype(bf16)
            if last > WINDOW:
                grad_pair[which, WINDOW:last, lanes] = mid[which, WINDOW:last, lanes].astype(bf16)
        return carry

    lax.fori_loop(0, pairs, combine, 0)
    launch(2, normed_t, grad_pair.at[0])
    launch(3, normed_t, grad_pair.at[1])
    advance(0, 1)
    advance(1, 1)
    advance(2, 0)
    advance(3, 0)
    for start in range(0, channels, strip):
        cols = slice(start, start + strip)
        more = dot(grad_pair[0], w_qkv[1, cols, :], ((1,), (1,)))
        more = more + dot(grad_pair[1], w_qkv[2, cols, :], ((1,), (1,)))
        grad_normed[:, cols] += more
    for stage in range(2, stages):
        advance(0, stage)
        advance(1, stage)
        if stage == 2:

            def norm_back(step, carry):
                rows = pl.ds(pl.multiple_of(step * few, few), few)
                unit, inverse = standardise(frames[rows, :].astype(f32))
                grad = grad_normed[rows, :].astype(bf16).astype(f32) * gain[...]
                average = jnp.mean(grad, axis=-1, keepdims=True)
                along = jnp.mean(grad * unit, axis=-1, keepdims=True)
                grad = inverse * (grad - average - unit * along)
                grad_frames[rows, :] = (cotangent[rows, :].astype(f32) + grad).astype(bf16)
                return carry

            lax.fori_loop(0, length // few, norm_back, 0)
        advance(2, stage - 1)
        advance(3, stage - 1)
    advance(2, stages - 1)
    advance(3, stages - 1)


def shards(frames, cotangent, norm_gain, w_qkv, w_out):
    length, channels = frames.shape
    seq_size, head_size = lax.axis_size("seq"), lax.axis_size("head")
    devices = seq_size * head_size
    bordered = length + 2 * WINDOW
    wide = 2 * HEAD_SIZE
    pairs = channels // wide
    tile_rows, tile_cols = channels // seq_size, channels // head_size
    outer = [("seq", bit) for bit in bits_of(seq_size)[1:]]
    along = [("head", bit) for bit in bits_of(head_size)]
    first = [("seq", 0)]
    orders = [
        first + outer + along,
        first + outer[::-1] + along,
        first + along[:1] + outer + along[1:],
        first + along[:1] + outer[::-1] + along[1:],
    ]
    chunks, stages = len(orders), len(orders[0])
    bf16, f32 = jnp.bfloat16, jnp.float32
    vmem, anywhere = pl.BlockSpec(memory_space=pltpu.VMEM), pl.BlockSpec(memory_space=pl.ANY)
    dma = pltpu.SemaphoreType.DMA
    output, grad_frames, grad_qkv, grad_out = pl.pallas_call(
        functools.partial(block_kernel, (seq_size, head_size), orders, (devices * length) ** (-0.5)),
        out_shape=[
            jax.ShapeDtypeStruct((length, channels), bf16),
            jax.ShapeDtypeStruct((length, channels), bf16),
            jax.ShapeDtypeStruct((3, tile_rows, tile_cols), f32),
            jax.ShapeDtypeStruct((tile_rows, tile_cols), f32),
        ],
        in_specs=[vmem, vmem, vmem, anywhere, anywhere],
        out_specs=[vmem] * 4,
        scratch_shapes=[
            pltpu.VMEM((3, channels, channels), bf16),
            pltpu.VMEM((channels, channels), bf16),
            pltpu.VMEM((bordered, channels), bf16),
            pltpu.VMEM((channels, length), bf16),
            pltpu.VMEM((length, channels), bf16),
            pltpu.VMEM((bordered, channels), bf16),
            pltpu.VMEM((bordered, channels), bf16),
            pltpu.VMEM((length, channels), bf16),
            pltpu.VMEM((length, channels), bf16),
            pltpu.VMEM((channels, length), bf16),
            pltpu.VMEM((length, channels), bf16),
            pltpu.VMEM((2, length, channels), f32),
            pltpu.VMEM((pairs, 2, 2, WINDOW, wide), bf16),
            pltpu.VMEM((pairs, 2, 2, WINDOW, wide), bf16),
            pltpu.VMEM((2, length, channels), bf16),
            pltpu.VMEM((length, channels), f32),
            pltpu.VMEM((chunks, devices, tile_rows, tile_cols), bf16),
            pltpu.VMEM((chunks, devices, tile_rows, tile_cols), bf16),
            pltpu.VMEM((2, WINDOW, channels), bf16),
            dma((4,)),
            dma((2,)),
            dma((2,)),
            dma((pairs, 2)),
            dma((pairs, 2)),
            dma((chunks, stages)),
            dma((chunks, stages)),
        ],
        compiler_params=pltpu.CompilerParams(
            collective_id=0, has_side_effects=True, vmem_limit_bytes=60 * 2**20
        ),
        name="block",
    )(frames, cotangent, norm_gain.reshape(1, channels), w_qkv, w_out)
    return (output, grad_frames, grad_qkv, grad_out)


def solution(mesh):
    in_specs = (P(("seq", "head"), None), P(("seq", "head"), None), P(), P(), P())
    out_specs = (
        P(("seq", "head"), None),
        P(("seq", "head"), None),
        P(None, "seq", "head"),
        P("seq", "head"),
    )
    return jax.shard_map(shards, mesh=mesh, in_specs=in_specs, out_specs=out_specs, check_vma=False)
```

```python
import functools

import jax
import jax.numpy as jnp
from jax import lax
from jax.experimental import pallas as pl
from jax.experimental.pallas import tpu as pltpu
from jax.sharding import PartitionSpec as P

HEAD_SIZE = 128
WINDOW = 128

EPSILON = 1e-05
MASKED = -1e30
AXES = ("seq", "head")


def dot(a, b, contract):
    return lax.dot_general(a, b, (contract, ((), ())), preferred_element_type=jnp.float32)


def bits_of(size):
    return list(range(size.bit_length() - 1))


def block_kernel(
    sizes, orders,
    frames, cotangent, gain, w_qkv_hbm, w_out_hbm,
    output, grad_frames, grad_qkv, grad_out,
    w_qkv, w_out, normed, normed_t, query, key, value, upstream, attended, attended_t,
    grad_query, grad_pair, shares, edge_out, edge_in, grad_normed, held, landed, halo,
    weight_sem, halo_send, halo_recv, edge_send, edge_recv, send_sem, recv_sem,
):
    seq_size, head_size = sizes
    devices = tiles = seq_size * head_size
    length, channels = frames.shape
    chunks, stages = len(orders), len(orders[0])
    tile_rows, tile_cols = held.shape[2:]
    place = {axis: lax.axis_index(axis) for axis in AXES}
    position = place["seq"] * head_size + place["head"]
    bf16, f32 = jnp.bfloat16, jnp.float32
    strip = min(256, channels)

    def neighbour(step):
        there = (position + step + devices) % devices
        return (there // head_size, there % head_size)

    def bit_at(order):
        axis, bit = order
        return (place[axis] // 2**bit) % 2

    def partner(order):
        axis, bit = order
        moved = place[axis] + (1 - 2 * bit_at(order)) * 2**bit
        return tuple(moved if name == axis else place[name] for name in AXES)

    weights = [pltpu.make_async_copy(w_out_hbm, w_out, weight_sem.at[3])]
    for which in range(3):
        weights.append(
            pltpu.make_async_copy(w_qkv_hbm.at[which], w_qkv.at[which], weight_sem.at[which])
        )
    for one in weights:
        one.start()

    greeted = [partner(order) for order in orders[0]] + [neighbour(1), neighbour(-1)]
    barrier = pltpu.get_barrier_semaphore()
    for device in greeted:
        pl.semaphore_signal(barrier, inc=1, device_id=device, device_id_type=pl.DeviceIdType.MESH)
    pl.semaphore_wait(barrier, len(greeted))

    def halo_copy(side):
        rows = pl.ds(length - WINDOW, WINDOW) if side == 0 else pl.ds(0, WINDOW)
        return pltpu.make_async_remote_copy(
            src_ref=frames.at[rows],
            dst_ref=halo.at[side],
            send_sem=halo_send.at[side],
            recv_sem=halo_recv.at[side],
            device_id=neighbour(1 if side == 0 else -1),
            device_id_type=pl.DeviceIdType.MESH,
        )

    halo_copy(0).start()
    halo_copy(1).start()

    def standardise(values):
        average = jnp.mean(values, axis=-1, keepdims=True)
        centered = values - average
        variance = jnp.mean(centered * centered, axis=-1, keepdims=True)
        inverse = lax.rsqrt(variance + EPSILON)
        return centered * inverse, inverse

    few = 64

    def norm_rows(source, target_row, rows):
        def one(step, carry):
            values = source[pl.ds(pl.multiple_of(step * few, few), few), :].astype(f32)
            rounded = (standardise(values)[0] * gain[...]).astype(bf16)
            normed[pl.ds(pl.multiple_of(target_row + step * few, few), few), :] = rounded
            return carry

        lax.fori_loop(0, rows // few, one, 0)

    def multiply_into(target, rows, left, weight, side):
        for start in range(0, channels, strip):
            cols = slice(start, start + strip)
            other = weight[:, cols] if side == 0 else weight[cols, :]
            target[rows, cols] = dot(left, other, ((1,), (side,))).astype(target.dtype)

    norm_rows(frames, WINDOW, length)
    own = slice(WINDOW, WINDOW + length)

    def turn(first, last):
        for start in range(first, last, 128):
            for col in range(0, channels, 128):
                tile = normed[start : start + 128, col : col + 128]
                normed_t[col : col + 128, start : start + 128] = tile.astype(f32).T.astype(bf16)

    turn(WINDOW, WINDOW + length)
    weights[0].wait()
    everything = slice(0, length)
    multiply_into(upstream, everything, cotangent[...], w_out, 1)
    for which, target, rows in ((0, query, everything), (1, key, own), (2, value, own)):
        weights[1 + which].wait()
        multiply_into(target, rows, normed[own, :], w_qkv.at[which], 0)
    for side in range(2):
        halo_copy(side).wait()
        start = side * (length + WINDOW)
        norm_rows(halo.at[side], start, WINDOW)
    for side in range(2):
        start = side * (length + WINDOW)
        rows = slice(start, start + WINDOW)
        multiply_into(key, rows, normed[rows, :], w_qkv.at[1], 0)
        multiply_into(value, rows, normed[rows, :], w_qkv.at[2], 0)

    wide = 2 * HEAD_SIZE
    pairs = channels // wide

    def edge_copy(side):
        return pltpu.make_async_remote_copy(
            src_ref=edge_out.at[side],
            dst_ref=edge_in.at[side],
            send_sem=edge_send.at[side],
            recv_sem=edge_recv.at[side],
            device_id=neighbour(-1 if side == 0 else 1),
            device_id_type=pl.DeviceIdType.MESH,
        )

    blocks = length // WINDOW
    span = 3 * WINDOW
    score_scale = HEAD_SIZE ** (-0.5)
    row = lax.broadcasted_iota(jnp.int32, (WINDOW, span), 0)
    col = lax.broadcasted_iota(jnp.int32, (WINDOW, span), 1)
    near = (col >= row) & (col <= row + 2 * WINDOW)

    def forward(pair, carry):
        for head in range(wide // HEAD_SIZE):
            lane = pl.multiple_of(pair * wide + head * HEAD_SIZE, HEAD_SIZE)
            lanes = pl.ds(lane, HEAD_SIZE)
            for block in range(blocks):
                rows = slice(block * WINDOW, (block + 1) * WINDOW)
                keys = slice(block * WINDOW, block * WINDOW + span)
                q, k, v = query[rows, lanes], key[keys, lanes], value[keys, lanes]
                frame = position * length + (block - 1) * WINDOW + col
                allowed = near & (frame >= 0) & (frame < devices * length)
                scores = jnp.where(allowed, dot(q, k, ((1,), (1,))) * score_scale, MASKED)
                share = jnp.exp(scores - jnp.max(scores, axis=-1, keepdims=True))
                share = (share * (1.0 / jnp.sum(share, axis=-1, keepdims=True))).astype(bf16)
                shares[pair * (wide // HEAD_SIZE) + head, block] = share
                mixed = dot(share, v, ((1,), (0,)))
                attended[rows, lanes] = mixed.astype(bf16)
                attended_t[lanes, rows] = mixed.T.astype(bf16)
        return carry

    def backward(pair, carry):
        for head in range(wide // HEAD_SIZE):
            lane = pl.multiple_of(pair * wide + head * HEAD_SIZE, HEAD_SIZE)
            lanes = pl.ds(lane, HEAD_SIZE)
            key_grads = [None] * (blocks + 2)
            value_grads = [None] * (blocks + 2)
            for block in range(blocks):
                rows = slice(block * WINDOW, (block + 1) * WINDOW)
                keys = slice(block * WINDOW, block * WINDOW + span)
                q, k, v, up = query[rows, lanes], key[keys, lanes], value[keys, lanes], upstream[rows, lanes]
                rounded = shares[pair * (wide // HEAD_SIZE) + head, block]
                share = rounded.astype(f32)
                grad = dot(up, v, ((1,), (1,)))
                centre = jnp.sum(share * grad, axis=-1, keepdims=True)
                grad = (share * (grad - centre) * score_scale).astype(bf16)
                grad_query[rows, lanes] = dot(grad, k, ((1,), (0,))).astype(bf16)
                key_grad = dot(grad, q, ((0,), (0,)))
                value_grad = dot(rounded, up, ((0,), (0,)))
                for part in range(3):
                    piece = slice(part * WINDOW, (part + 1) * WINDOW)
                    for sums, term in ((key_grads, key_grad[piece]), (value_grads, value_grad[piece])):
                        before = sums[block + part]
                        sums[block + part] = term if before is None else before + term
            for which, sums in enumerate((key_grads, value_grads)):
                for block in range(blocks + 2):
                    rows = slice(block * WINDOW, (block + 1) * WINDOW)
                    grad_pair[which, rows, lanes] = sums[block].astype(bf16)
        return carry

    def base(chunk, stage):
        total = 0
        for step in range(stage):
            total = total + bit_at(orders[chunk][step]) * (tiles >> (step + 1))
        return total

    def landing(stage):
        return tiles - (tiles >> stage)

    def copy(chunk, stage):
        half = tiles >> (stage + 1)
        order = orders[chunk][stage]
        other = base(chunk, stage) + (1 - bit_at(order)) * half
        return pltpu.make_async_remote_copy(
            src_ref=held.at[chunk, pl.ds(other, half)],
            dst_ref=landed.at[chunk, pl.ds(landing(stage), half)],
            send_sem=send_sem.at[chunk, stage],
            recv_sem=recv_sem.at[chunk, stage],
            device_id=partner(order),
            device_id_type=pl.DeviceIdType.MESH,
        )

    def advance(chunk, stage):
        copy(chunk, stage).wait()
        half = tiles >> (stage + 1)
        keep = base(chunk, stage + 1)
        if stage == stages - 1:
            total = held[chunk, keep].astype(f32) + landed[chunk, landing(stage)].astype(f32)
            if chunk == 0:
                grad_out[...] = total
            else:
                grad_qkv[chunk - 1] = total
            return

        def add(step, carry):
            total = held[chunk, keep + step].astype(f32) + landed[chunk, landing(stage) + step].astype(f32)
            held[chunk, keep + step] = total.astype(bf16)
            return carry

        lax.fori_loop(0, half, add, 0)
        copy(chunk, stage + 1).start()

    def tile_place(chunk, axis, index):
        total = 0
        for step, (name, bit) in enumerate(orders[chunk]):
            if name == axis:
                total = total + ((index // 2**bit) % 2) * (tiles >> (step + 1))
        return total

    def products(chunk, left, right, depth, half):
        def one(step, carry):
            block = 2 * step + half
            rows = pl.ds(pl.multiple_of(block * tile_rows, tile_rows), tile_rows)
            product = dot(left[rows, depth], right[...], ((1,), (0,))).astype(bf16)
            down = tile_place(chunk, "seq", block)
            for col in range(head_size):
                held[chunk, down + tile_place(chunk, "head", col)] = product[
                    :, col * tile_cols : (col + 1) * tile_cols
                ]
            return carry

        lax.fori_loop(0, seq_size // 2, one, 0)

    def launch(chunk, left, right, depth):
        mine = bit_at(orders[chunk][0])
        products(chunk, left, right, depth, 1 - mine)
        copy(chunk, 0).start()
        products(chunk, left, right, depth, mine)

    lax.fori_loop(0, pairs, forward, 0)
    launch(0, attended_t, cotangent, everything)
    lax.fori_loop(0, pairs // 2, backward, 0)
    advance(0, 0)
    lax.fori_loop(pairs // 2, pairs, backward, 0)
    launch(1, normed_t, grad_query, own)
    turn(0, WINDOW)
    turn(WINDOW + length, 2 * WINDOW + length)
    launch(2, normed_t, grad_pair.at[0], slice(0, 2 * WINDOW + length))
    advance(1, 0)
    launch(3, normed_t, grad_pair.at[1], slice(0, 2 * WINDOW + length))
    advance(2, 0)

    def pair_back(rows, cols):
        term = dot(grad_pair[0, rows, :], w_qkv[1, cols, :], ((1,), (1,)))
        return term + dot(grad_pair[1, rows, :], w_qkv[2, cols, :], ((1,), (1,)))

    for side in range(2):
        start = side * (length + WINDOW)
        for strip_start in range(0, channels, strip):
            cols = slice(strip_start, strip_start + strip)
            edge_out[side, :, cols] = pair_back(slice(start, start + WINDOW), cols).astype(bf16)
        edge_copy(side).start()
    advance(3, 0)
    for start in range(0, channels, strip):
        cols = slice(start, start + strip)
        mixed = dot(attended[...], w_out[:, cols], ((1,), (0,)))
        output[:, cols] = (frames[:, cols].astype(f32) + mixed).astype(bf16)
    advance(0, 1)
    for start in range(0, channels, strip):
        cols = slice(start, start + strip)
        grad_normed[:, cols] = pair_back(own, cols) + dot(grad_query[...], w_qkv[0, cols, :], ((1,), (1,)))
    advance(1, 1)
    advance(2, 1)
    advance(3, 1)

    def norm_back(step, carry):
        rows = pl.ds(pl.multiple_of(step * few, few), few)
        unit, inverse = standardise(frames[rows, :].astype(f32))
        grad = grad_normed[rows, :].astype(bf16).astype(f32) * gain[...]
        average = jnp.mean(grad, axis=-1, keepdims=True)
        along = jnp.mean(grad * unit, axis=-1, keepdims=True)
        grad = inverse * (grad - average - unit * along)
        grad_frames[rows, :] = (cotangent[rows, :].astype(f32) + grad).astype(bf16)
        return carry

    for stage in range(2, stages):
        for chunk in range(chunks):
            advance(chunk, stage)
        if stage == 2:
            edge_copy(0).wait()
            edge_copy(1).wait()
            grad_normed[:WINDOW, :] += edge_in[1].astype(f32)
            grad_normed[length - WINDOW :, :] += edge_in[0].astype(f32)
            lax.fori_loop(0, length // few, norm_back, 0)


def deliver_kernel(scale, output, grad_frames, grad_qkv, grad_out, *targets):
    targets[0][...] = output[...]
    targets[1][...] = grad_frames[...]
    targets[2][...] = grad_qkv[...] * scale
    targets[3][...] = grad_out[...] * scale


def shards(frames, cotangent, norm_gain, w_qkv, w_out):
    length, channels = frames.shape
    seq_size, head_size = lax.axis_size("seq"), lax.axis_size("head")
    devices = seq_size * head_size
    bordered = length + 2 * WINDOW
    tile_rows, tile_cols = channels // seq_size, channels // head_size
    outer = [("seq", bit) for bit in bits_of(seq_size)[1:]]
    along = [("head", bit) for bit in bits_of(head_size)]
    first = [("seq", 0)]
    orders = [
        first + outer + along,
        first + outer[::-1] + along,
        first + along[:1] + outer[::-1] + along[1:],
        first + outer[:1] + along[:1] + outer[1:] + along[1:],
    ]
    chunks, stages = len(orders), len(orders[0])
    bf16, f32 = jnp.bfloat16, jnp.float32
    vmem, anywhere = pl.BlockSpec(memory_space=pltpu.VMEM), pl.BlockSpec(memory_space=pl.ANY)
    dma = pltpu.SemaphoreType.DMA
    shapes = [
        jax.ShapeDtypeStruct((length, channels), bf16),
        jax.ShapeDtypeStruct((length, channels), bf16),
        jax.ShapeDtypeStruct((3, tile_rows, tile_cols), f32),
        jax.ShapeDtypeStruct((tile_rows, tile_cols), f32),
    ]
    results = pl.pallas_call(
        functools.partial(block_kernel, (seq_size, head_size), orders),
        out_shape=shapes,
        in_specs=[vmem, vmem, vmem, anywhere, anywhere],
        out_specs=[vmem] * 4,
        scratch_shapes=[
            pltpu.VMEM((3, channels, channels), bf16),
            pltpu.VMEM((channels, channels), bf16),
            pltpu.VMEM((bordered, channels), bf16),
            pltpu.VMEM((channels, bordered), bf16),
            pltpu.VMEM((length, channels), bf16),
            pltpu.VMEM((bordered, channels), bf16),
            pltpu.VMEM((bordered, channels), bf16),
            pltpu.VMEM((length, channels), bf16),
            pltpu.VMEM((length, channels), bf16),
            pltpu.VMEM((channels, length), bf16),
            pltpu.VMEM((length, channels), bf16),
            pltpu.VMEM((2, bordered, channels), bf16),
            pltpu.VMEM((channels // HEAD_SIZE, length // WINDOW, WINDOW, 3 * WINDOW), bf16),
            pltpu.VMEM((2, WINDOW, channels), bf16),
            pltpu.VMEM((2, WINDOW, channels), bf16),
            pltpu.VMEM((length, channels), f32),
            pltpu.VMEM((chunks, devices, tile_rows, tile_cols), bf16),
            pltpu.VMEM((chunks, devices, tile_rows, tile_cols), bf16),
            pltpu.VMEM((2, WINDOW, channels), bf16),
            dma((4,)),
            dma((2,)),
            dma((2,)),
            dma((2,)),
            dma((2,)),
            dma((chunks, stages)),
            dma((chunks, stages)),
        ],
        compiler_params=pltpu.CompilerParams(
            collective_id=0, has_side_effects=True, vmem_limit_bytes=60 * 2**20
        ),
        name="block",
    )(frames, cotangent, norm_gain.reshape(1, channels), w_qkv, w_out)
    return tuple(
        pl.pallas_call(
            functools.partial(deliver_kernel, (devices * length) ** (-0.5)),
            out_shape=shapes,
            in_specs=[vmem] * 4,
            out_specs=[vmem] * 4,
            name="deliver",
        )(*results)
    )


def solution(mesh):
    in_specs = (P(("seq", "head"), None), P(("seq", "head"), None), P(), P(), P())
    out_specs = (
        P(("seq", "head"), None),
        P(("seq", "head"), None),
        P(None, "seq", "head"),
        P("seq", "head"),
    )
    return jax.shard_map(shards, mesh=mesh, in_specs=in_specs, out_specs=out_specs, check_vma=False)
```

```python
import functools

import jax
import jax.numpy as jnp
from jax import lax
from jax.experimental import pallas as pl
from jax.experimental.pallas import tpu as pltpu
from jax.sharding import PartitionSpec as P

HEAD_SIZE = 128
WINDOW = 128

EPSILON = 1e-05
MASKED = -1e30
AXES = ("seq", "head")


def dot(a, b, contract):
    return lax.dot_general(a, b, (contract, ((), ())), preferred_element_type=jnp.float32)


def bits_of(size):
    return list(range(size.bit_length() - 1))


def block_kernel(
    sizes, orders,
    frames, cotangent, gain, w_qkv_hbm, w_out_hbm,
    output, grad_frames, grad_qkv, grad_out,
    w_qkv, w_out, normed, normed_t, query, key, value, upstream, attended, attended_t,
    grad_query, grad_pair, shares, edge_out, edge_in, grad_normed, held, landed, halo,
    weight_sem, halo_send, halo_recv, edge_send, edge_recv, send_sem, recv_sem,
):
    seq_size, head_size = sizes
    devices = tiles = seq_size * head_size
    length, channels = frames.shape
    chunks, stages = len(orders), len(orders[0])
    tile_rows, tile_cols = held.shape[2:]
    place = {axis: lax.axis_index(axis) for axis in AXES}
    position = place["seq"] * head_size + place["head"]
    bf16, f32 = jnp.bfloat16, jnp.float32
    strip = min(256, channels)

    def neighbour(step):
        there = (position + step + devices) % devices
        return (there // head_size, there % head_size)

    def bit_at(order):
        axis, bit = order
        return (place[axis] // 2**bit) % 2

    def partner(order):
        axis, bit = order
        moved = place[axis] + (1 - 2 * bit_at(order)) * 2**bit
        return tuple(moved if name == axis else place[name] for name in AXES)

    weights = [pltpu.make_async_copy(w_out_hbm, w_out, weight_sem.at[3])]
    for which in range(3):
        weights.append(
            pltpu.make_async_copy(w_qkv_hbm.at[which], w_qkv.at[which], weight_sem.at[which])
        )
    for one in weights:
        one.start()

    greeted = [partner(order) for order in orders[0]] + [neighbour(1), neighbour(-1)]
    barrier = pltpu.get_barrier_semaphore()
    for device in greeted:
        pl.semaphore_signal(barrier, inc=1, device_id=device, device_id_type=pl.DeviceIdType.MESH)
    pl.semaphore_wait(barrier, len(greeted))

    def halo_copy(side):
        rows = pl.ds(length - WINDOW, WINDOW) if side == 0 else pl.ds(0, WINDOW)
        return pltpu.make_async_remote_copy(
            src_ref=frames.at[rows],
            dst_ref=halo.at[side],
            send_sem=halo_send.at[side],
            recv_sem=halo_recv.at[side],
            device_id=neighbour(1 if side == 0 else -1),
            device_id_type=pl.DeviceIdType.MESH,
        )

    halo_copy(0).start()
    halo_copy(1).start()

    def standardise(values):
        average = jnp.mean(values, axis=-1, keepdims=True)
        centered = values - average
        variance = jnp.mean(centered * centered, axis=-1, keepdims=True)
        inverse = lax.rsqrt(variance + EPSILON)
        return centered * inverse, inverse

    few = 64

    def norm_rows(source, target_row, rows):
        def one(step, carry):
            values = source[pl.ds(pl.multiple_of(step * few, few), few), :].astype(f32)
            rounded = (standardise(values)[0] * gain[...]).astype(bf16)
            normed[pl.ds(pl.multiple_of(target_row + step * few, few), few), :] = rounded
            return carry

        lax.fori_loop(0, rows // few, one, 0)

    def multiply_into(target, rows, left, weight, side):
        for start in range(0, channels, strip):
            cols = slice(start, start + strip)
            other = weight[:, cols] if side == 0 else weight[cols, :]
            target[rows, cols] = dot(left, other, ((1,), (side,))).astype(target.dtype)

    norm_rows(frames, WINDOW, length)
    own = slice(WINDOW, WINDOW + length)

    def turn(first, last):
        for start in range(first, last, 128):
            for col in range(0, channels, 128):
                tile = normed[start : start + 128, col : col + 128]
                normed_t[col : col + 128, start : start + 128] = tile.astype(f32).T.astype(bf16)

    turn(WINDOW, WINDOW + length)
    weights[0].wait()
    everything = slice(0, length)
    multiply_into(upstream, everything, cotangent[...], w_out, 1)
    for which, target, rows in ((0, query, everything), (1, key, own), (2, value, own)):
        weights[1 + which].wait()
        multiply_into(target, rows, normed[own, :], w_qkv.at[which], 0)
    for side in range(2):
        halo_copy(side).wait()
        start = side * (length + WINDOW)
        norm_rows(halo.at[side], start, WINDOW)
    for side in range(2):
        start = side * (length + WINDOW)
        rows = slice(start, start + WINDOW)
        multiply_into(key, rows, normed[rows, :], w_qkv.at[1], 0)
        multiply_into(value, rows, normed[rows, :], w_qkv.at[2], 0)

    wide = 2 * HEAD_SIZE
    pairs = channels // wide

    def edge_copy(side):
        return pltpu.make_async_remote_copy(
            src_ref=edge_out.at[side],
            dst_ref=edge_in.at[side],
            send_sem=edge_send.at[side],
            recv_sem=edge_recv.at[side],
            device_id=neighbour(-1 if side == 0 else 1),
            device_id_type=pl.DeviceIdType.MESH,
        )

    blocks = length // WINDOW
    span = 3 * WINDOW
    score_scale = HEAD_SIZE ** (-0.5)
    row = lax.broadcasted_iota(jnp.int32, (WINDOW, span), 0)
    col = lax.broadcasted_iota(jnp.int32, (WINDOW, span), 1)
    near = (col >= row) & (col <= row + 2 * WINDOW)

    def forward(pair, carry):
        for head in range(wide // HEAD_SIZE):
            lane = pl.multiple_of(pair * wide + head * HEAD_SIZE, HEAD_SIZE)
            lanes = pl.ds(lane, HEAD_SIZE)
            for block in range(blocks):
                rows = slice(block * WINDOW, (block + 1) * WINDOW)
                keys = slice(block * WINDOW, block * WINDOW + span)
                q, k, v = query[rows, lanes], key[keys, lanes], value[keys, lanes]
                frame = position * length + (block - 1) * WINDOW + col
                allowed = near & (frame >= 0) & (frame < devices * length)
                scores = jnp.where(allowed, dot(q, k, ((1,), (1,))) * score_scale, MASKED)
                share = jnp.exp(scores - jnp.max(scores, axis=-1, keepdims=True))
                share = (share * (1.0 / jnp.sum(share, axis=-1, keepdims=True))).astype(bf16)
                shares[pair * (wide // HEAD_SIZE) + head, block] = share
                mixed = dot(share, v, ((1,), (0,)))
                attended[rows, lanes] = mixed.astype(bf16)
                attended_t[lanes, rows] = mixed.T.astype(bf16)
        return carry

    def backward(pair, carry):
        for head in range(wide // HEAD_SIZE):
            lane = pl.multiple_of(pair * wide + head * HEAD_SIZE, HEAD_SIZE)
            lanes = pl.ds(lane, HEAD_SIZE)
            key_grads = [None] * (blocks + 2)
            value_grads = [None] * (blocks + 2)
            for block in range(blocks):
                rows = slice(block * WINDOW, (block + 1) * WINDOW)
                keys = slice(block * WINDOW, block * WINDOW + span)
                q, k, v, up = query[rows, lanes], key[keys, lanes], value[keys, lanes], upstream[rows, lanes]
                rounded = shares[pair * (wide // HEAD_SIZE) + head, block]
                share = rounded.astype(f32)
                grad = dot(up, v, ((1,), (1,)))
                centre = jnp.sum(share * grad, axis=-1, keepdims=True)
                grad = (share * (grad - centre) * score_scale).astype(bf16)
                grad_query[rows, lanes] = dot(grad, k, ((1,), (0,))).astype(bf16)
                key_grad = dot(grad, q, ((0,), (0,)))
                value_grad = dot(rounded, up, ((0,), (0,)))
                for part in range(3):
                    piece = slice(part * WINDOW, (part + 1) * WINDOW)
                    for sums, term in ((key_grads, key_grad[piece]), (value_grads, value_grad[piece])):
                        before = sums[block + part]
                        sums[block + part] = term if before is None else before + term
            for which, sums in enumerate((key_grads, value_grads)):
                for block in range(blocks + 2):
                    rows = slice(block * WINDOW, (block + 1) * WINDOW)
                    grad_pair[which, rows, lanes] = sums[block].astype(bf16)
        return carry

    def base(chunk, stage):
        total = 0
        for step in range(stage):
            total = total + bit_at(orders[chunk][step]) * (tiles >> (step + 1))
        return total

    def landing(stage):
        return tiles - (tiles >> stage)

    def copy(chunk, stage):
        half = tiles >> (stage + 1)
        order = orders[chunk][stage]
        other = base(chunk, stage) + (1 - bit_at(order)) * half
        return pltpu.make_async_remote_copy(
            src_ref=held.at[chunk, pl.ds(other, half)],
            dst_ref=landed.at[chunk, pl.ds(landing(stage), half)],
            send_sem=send_sem.at[chunk, stage],
            recv_sem=recv_sem.at[chunk, stage],
            device_id=partner(order),
            device_id_type=pl.DeviceIdType.MESH,
        )

    def advance(chunk, stage):
        copy(chunk, stage).wait()
        half = tiles >> (stage + 1)
        keep = base(chunk, stage + 1)
        if stage == stages - 1:
            total = held[chunk, keep].astype(f32) + landed[chunk, landing(stage)].astype(f32)
            if chunk == 0:
                grad_out[...] = total
            else:
                grad_qkv[chunk - 1] = total
            return

        def add(step, carry):
            total = held[chunk, keep + step].astype(f32) + landed[chunk, landing(stage) + step].astype(f32)
            held[chunk, keep + step] = total.astype(bf16)
            return carry

        lax.fori_loop(0, half, add, 0)
        copy(chunk, stage + 1).start()

    def tile_place(chunk, axis, index):
        total = 0
        for step, (name, bit) in enumerate(orders[chunk]):
            if name == axis:
                total = total + ((index // 2**bit) % 2) * (tiles >> (step + 1))
        return total

    def products(chunk, left, right, depth, half):
        def one(step, carry):
            block = 2 * step + half
            rows = pl.ds(pl.multiple_of(block * tile_rows, tile_rows), tile_rows)
            product = dot(left[rows, depth], right[...], ((1,), (0,))).astype(bf16)
            down = tile_place(chunk, "seq", block)
            for col in range(head_size):
                held[chunk, down + tile_place(chunk, "head", col)] = product[
                    :, col * tile_cols : (col + 1) * tile_cols
                ]
            return carry

        lax.fori_loop(0, seq_size // 2, one, 0)

    def launch(chunk, left, right, depth):
        mine = bit_at(orders[chunk][0])
        products(chunk, left, right, depth, 1 - mine)
        copy(chunk, 0).start()
        products(chunk, left, right, depth, mine)

    lax.fori_loop(0, pairs, forward, 0)
    launch(0, attended_t, cotangent, everything)
    lax.fori_loop(0, pairs // 2, backward, 0)
    advance(0, 0)
    lax.fori_loop(pairs // 2, pairs, backward, 0)
    launch(1, normed_t, grad_query, own)
    turn(0, WINDOW)
    turn(WINDOW + length, 2 * WINDOW + length)
    launch(2, normed_t, grad_pair.at[0], slice(0, 2 * WINDOW + length))
    advance(1, 0)
    launch(3, normed_t, grad_pair.at[1], slice(0, 2 * WINDOW + length))
    advance(0, 1)
    advance(2, 0)
    advance(3, 0)

    def pair_back(rows, cols):
        term = dot(grad_pair[0, rows, :], w_qkv[1, cols, :], ((1,), (1,)))
        return term + dot(grad_pair[1, rows, :], w_qkv[2, cols, :], ((1,), (1,)))

    for side in range(2):
        start = side * (length + WINDOW)
        for strip_start in range(0, channels, strip):
            cols = slice(strip_start, strip_start + strip)
            edge_out[side, :, cols] = pair_back(slice(start, start + WINDOW), cols).astype(bf16)
        edge_copy(side).start()
    for start in range(0, channels, strip):
        cols = slice(start, start + strip)
        mixed = dot(attended[...], w_out[:, cols], ((1,), (0,)))
        output[:, cols] = (frames[:, cols].astype(f32) + mixed).astype(bf16)
    advance(1, 1)
    advance(0, 2)
    for start in range(0, channels, strip):
        cols = slice(start, start + strip)
        grad_normed[:, cols] = pair_back(own, cols) + dot(grad_query[...], w_qkv[0, cols, :], ((1,), (1,)))
    advance(2, 1)
    advance(3, 1)

    def norm_back(step, carry):
        rows = pl.ds(pl.multiple_of(step * few, few), few)
        unit, inverse = standardise(frames[rows, :].astype(f32))
        grad = grad_normed[rows, :].astype(bf16).astype(f32) * gain[...]
        average = jnp.mean(grad, axis=-1, keepdims=True)
        along = jnp.mean(grad * unit, axis=-1, keepdims=True)
        grad = inverse * (grad - average - unit * along)
        grad_frames[rows, :] = (cotangent[rows, :].astype(f32) + grad).astype(bf16)
        return carry

    for stage in range(2, stages):
        for chunk in range(1 if stage == 2 else 0, chunks):
            advance(chunk, stage)
        if stage == 2:
            edge_copy(0).wait()
            edge_copy(1).wait()
            grad_normed[:WINDOW, :] += edge_in[1].astype(f32)
            grad_normed[length - WINDOW :, :] += edge_in[0].astype(f32)
            lax.fori_loop(0, length // few, norm_back, 0)


def deliver_kernel(scale, output, grad_frames, grad_qkv, grad_out, *targets):
    targets[0][...] = output[...]
    targets[1][...] = grad_frames[...]
    targets[2][...] = grad_qkv[...] * scale
    targets[3][...] = grad_out[...] * scale


def shards(frames, cotangent, norm_gain, w_qkv, w_out):
    length, channels = frames.shape
    seq_size, head_size = lax.axis_size("seq"), lax.axis_size("head")
    devices = seq_size * head_size
    bordered = length + 2 * WINDOW
    tile_rows, tile_cols = channels // seq_size, channels // head_size
    outer = [("seq", bit) for bit in bits_of(seq_size)[1:]]
    along = [("head", bit) for bit in bits_of(head_size)]
    first = [("seq", 0)]
    orders = [
        first + outer + along,
        first + outer[::-1] + along,
        first + along[:1] + outer[::-1] + along[1:],
        first + outer[:1] + along[:1] + outer[1:] + along[1:],
    ]
    chunks, stages = len(orders), len(orders[0])
    bf16, f32 = jnp.bfloat16, jnp.float32
    vmem, anywhere = pl.BlockSpec(memory_space=pltpu.VMEM), pl.BlockSpec(memory_space=pl.ANY)
    dma = pltpu.SemaphoreType.DMA
    shapes = [
        jax.ShapeDtypeStruct((length, channels), bf16),
        jax.ShapeDtypeStruct((length, channels), bf16),
        jax.ShapeDtypeStruct((3, tile_rows, tile_cols), f32),
        jax.ShapeDtypeStruct((tile_rows, tile_cols), f32),
    ]
    results = pl.pallas_call(
        functools.partial(block_kernel, (seq_size, head_size), orders),
        out_shape=shapes,
        in_specs=[vmem, vmem, vmem, anywhere, anywhere],
        out_specs=[vmem] * 4,
        scratch_shapes=[
            pltpu.VMEM((3, channels, channels), bf16),
            pltpu.VMEM((channels, channels), bf16),
            pltpu.VMEM((bordered, channels), bf16),
            pltpu.VMEM((channels, bordered), bf16),
            pltpu.VMEM((length, channels), bf16),
            pltpu.VMEM((bordered, channels), bf16),
            pltpu.VMEM((bordered, channels), bf16),
            pltpu.VMEM((length, channels), bf16),
            pltpu.VMEM((length, channels), bf16),
            pltpu.VMEM((channels, length), bf16),
            pltpu.VMEM((length, channels), bf16),
            pltpu.VMEM((2, bordered, channels), bf16),
            pltpu.VMEM((channels // HEAD_SIZE, length // WINDOW, WINDOW, 3 * WINDOW), bf16),
            pltpu.VMEM((2, WINDOW, channels), bf16),
            pltpu.VMEM((2, WINDOW, channels), bf16),
            pltpu.VMEM((length, channels), f32),
            pltpu.VMEM((chunks, devices, tile_rows, tile_cols), bf16),
            pltpu.VMEM((chunks, devices, tile_rows, tile_cols), bf16),
            pltpu.VMEM((2, WINDOW, channels), bf16),
            dma((4,)),
            dma((2,)),
            dma((2,)),
            dma((2,)),
            dma((2,)),
            dma((chunks, stages)),
            dma((chunks, stages)),
        ],
        compiler_params=pltpu.CompilerParams(
            collective_id=0, has_side_effects=True, vmem_limit_bytes=60 * 2**20
        ),
        name="block",
    )(frames, cotangent, norm_gain.reshape(1, channels), w_qkv, w_out)
    return tuple(
        pl.pallas_call(
            functools.partial(deliver_kernel, (devices * length) ** (-0.5)),
            out_shape=shapes,
            in_specs=[vmem] * 4,
            out_specs=[vmem] * 4,
            name="deliver",
        )(*results)
    )


def solution(mesh):
    in_specs = (P(("seq", "head"), None), P(("seq", "head"), None), P(), P(), P())
    out_specs = (
        P(("seq", "head"), None),
        P(("seq", "head"), None),
        P(None, "seq", "head"),
        P("seq", "head"),
    )
    return jax.shard_map(shards, mesh=mesh, in_specs=in_specs, out_specs=out_specs, check_vma=False)
```
